32 devices in a mesh: dom: 8 (over z, y), grp: 4 (over x, core).
Axes of the slice: x: 2, y: 2, z: 4, core: 2. Of those that a mesh axis runs over, the one named last changes fastest.
Arguments:
- nodes: bfloat16 [4, 4096, 128], P('grp', 'dom'), may hold values from -6 to 6
- edges: bfloat16 [4, 32, 128, 128], P('grp', 'dom'), may hold values from -6 to 6
- senders: int32 [4, 32, 128], P('grp', 'dom'), may hold values from 0 to 767
- receivers: int32 [4, 32, 128], P('grp', 'dom'), may hold values from 0 to 511
- block_count: int32 [4, 8], P('grp', 'dom'), may hold values from 1 to 4
- send_rows: int32 [4, 8, 2, 128], P('grp', 'dom'), may hold values from 0 to 511
- node_cot: bfloat16 [4, 4096, 128], P('grp', 'dom'), may hold values from -6 to 6
- edge_cot: bfloat16 [4, 32, 128, 128], P('grp', 'dom'), may hold values from -6 to 6
- edge_w1: bfloat16 [384, 128], replicated, may hold values from -0.3125 to 0.3125
- edge_b1: float32 [128], replicated, may hold values from -3 to 3
- edge_w2: bfloat16 [128, 128], replicated, may hold values from -0.5 to 0.5
- edge_b2: float32 [128], replicated, may hold values from -3 to 3
- edge_gain: float32 [128], replicated, may hold values from 0.5 to 1.5
- edge_shift: float32 [128], replicated, may hold values from -3 to 3
- node_w1: bfloat16 [256, 128], replicated, may hold values from -0.375 to 0.375
- node_b1: float32 [128], replicated, may hold values from -3 to 3
- node_w2: bfloat16 [128, 128], replicated, may hold values from -0.5 to 0.5
- node_b2: float32 [128], replicated, may hold values from -3 to 3
- node_gain: float32 [128], replicated, may hold values from 0.5 to 1.5
- node_shift: float32 [128], replicated, may hold values from -3 to 3
Outputs:
- node_out: bfloat16 [4, 4096, 128], P('grp', 'dom')
- edge_out: bfloat16 [4, 32, 128, 128], P('grp', 'dom')
- grad_node: bfloat16 [4, 4096, 128], P('grp', 'dom')
- grad_edge: bfloat16 [4, 32, 128, 128], P('grp', 'dom')
- weight_grads: float32 [115712], replicated
The draws below stay inside these ranges and needn't reach their ends.
Inputs may be any that keep to these rules, and one draw needn't show every extreme that they name: `senders`: rows below 512 are the device's own nodes; row 512 + k holds the k-th row sent by the lower neighbouring partition, row 640 + k the k-th row sent by the upper one. `receivers`: receivers are own nodes of the device that holds the edge. `block_count`: A device's live blocks are its first ones; the rest are padding. send_rows[g, d, 0, :] are own rows of device d sent to device d - 1 of group g, send_rows[g, d, 1, :] those sent to device d + 1; they may repeat; lists toward no device are unused.
All inputs are finite; a program needn't handle non-finite values.
Results may differ from the reference program's by a relative error of at most 0.0054.
Values may be sent and summed in bfloat16 or wider, within the bound.
A program may use at most 64 MiB of HBM per device.

```python
import math
import jax
import jax.numpy as jnp
from jax import lax

LAT = 128
HID = 128
NODE_DEV = 512
BLOCKS = 4
EBLOCK = 128
SLOTS = 128
GROUPS = 4
NODES = 4096
EDGE_BLOCKS = 32
N_DOM = 8
N_GRP = 4


def touch_ends(array, own_key, low, top_value):
    index_at = [jax.random.randint(jax.random.fold_in(own_key, axis), (), 0, length) for axis, length in enumerate(array.shape)]
    main_axis = array.shape.index(max(array.shape))
    neighbour = index_at[:main_axis] + [(index_at[main_axis] + 1) % array.shape[main_axis]] + index_at[main_axis + 1:]
    return array.at[tuple(index_at)].set(low).at[tuple(neighbour)].set(top_value)


def steps_of(key, dims, split, smallest, high):
    def one(position, shards_of):
        steps = jax.random.uniform(jax.random.fold_in(jax.random.fold_in(key, 6), position), (shards_of,), jnp.float32, smallest / len(split), high / len(split))
        return jnp.repeat(jnp.exp(steps), dims[position] // shards_of).reshape((-1,) + (1,) * (len(dims) - position - 1))

    factor_of = one(*split[0])
    for cut in split[1:]:
        factor_of = factor_of * one(*cut)
    return factor_of


def bell_draw(own_key, dims, scale, reach, pieces=(), kind=jnp.bfloat16):
    drawn = jax.random.normal(own_key, dims, jnp.float32) * scale
    if len(pieces) > 0:
        drawn = steps_of(own_key, dims, pieces, -0.22, 0.18) * drawn
    return jnp.clip(drawn, min=-reach, max=reach).astype(kind)


def setup_inputs(seed: int = 0) -> dict:
    arg_keys = jax.random.split(jax.random.key(seed), 21)
    nodes = bell_draw(arg_keys[0], (GROUPS, NODES, LAT), 1.0, 6.0, ((0, 4), (1, 8)))
    edges = bell_draw(arg_keys[1], (GROUPS, EDGE_BLOCKS, EBLOCK, LAT), 1.0, 6.0, ((0, 4), (1, 8)))
    senders = touch_ends(jax.random.randint(arg_keys[2], (GROUPS, EDGE_BLOCKS, EBLOCK), 0, NODE_DEV + 2 * SLOTS), jax.random.fold_in(arg_keys[2], 1), 0, (NODE_DEV + 2 * SLOTS) - 1).astype(jnp.int32)
    receivers = touch_ends(jax.random.randint(arg_keys[3], (GROUPS, EDGE_BLOCKS, EBLOCK), 0, NODE_DEV), jax.random.fold_in(arg_keys[3], 1), 0, NODE_DEV - 1).astype(jnp.int32)
    block_count = touch_ends(jax.random.randint(arg_keys[4], (GROUPS, N_DOM), max(1, BLOCKS // 4), BLOCKS + 1), jax.random.fold_in(arg_keys[4], 1), max(1, BLOCKS // 4), BLOCKS).astype(jnp.int32)
    send_rows = touch_ends(jax.random.randint(arg_keys[5], (GROUPS, N_DOM, 2, SLOTS), 0, NODE_DEV), jax.random.fold_in(arg_keys[5], 1), 0, NODE_DEV - 1).astype(jnp.int32)
    node_cot = bell_draw(arg_keys[6], (GROUPS, NODES, LAT), 1.0, 6.0, ((0, 4), (1, 8)))
    edge_cot = bell_draw(arg_keys[7], (GROUPS, EDGE_BLOCKS, EBLOCK, LAT), 1.0, 6.0, ((0, 4), (1, 8)))
    edge_w1 = bell_draw(arg_keys[8], (3 * LAT, HID), (3 * LAT) ** -0.5, 0.3125)
    edge_b1 = bell_draw(arg_keys[9], (HID,), 0.5, 3.0, (), jnp.float32)
    edge_w2 = bell_draw(arg_keys[10], (HID, LAT), HID ** -0.5, 0.5)
    edge_b2 = bell_draw(arg_keys[11], (LAT,), 0.5, 3.0, (), jnp.float32)
    edge_gain = jnp.clip(1.0 + 0.1 * jax.random.normal(arg_keys[12], (LAT,), jnp.float32), 0.5, 1.5)
    edge_shift = bell_draw(arg_keys[13], (LAT,), 0.5, 3.0, (), jnp.float32)
    node_w1 = bell_draw(arg_keys[14], (2 * LAT, HID), (2 * LAT) ** -0.5, 0.375)
    node_b1 = bell_draw(arg_keys[15], (HID,), 0.5, 3.0, (), jnp.float32)
    node_w2 = bell_draw(arg_keys[16], (HID, LAT), HID ** -0.5, 0.5)
    node_b2 = bell_draw(arg_keys[17], (LAT,), 0.5, 3.0, (), jnp.float32)
    node_gain = jnp.clip(1.0 + 0.1 * jax.random.normal(arg_keys[18], (LAT,), jnp.float32), 0.5, 1.5)
    node_shift = bell_draw(arg_keys[19], (LAT,), 0.5, 3.0, (), jnp.float32)
    return dict(nodes=nodes, edges=edges, senders=senders, receivers=receivers, block_count=block_count, send_rows=send_rows, node_cot=node_cot, edge_cot=edge_cot, edge_w1=edge_w1, edge_b1=edge_b1, edge_w2=edge_w2, edge_b2=edge_b2, edge_gain=edge_gain, edge_shift=edge_shift, node_w1=node_w1, node_b1=node_b1, node_w2=node_w2, node_b2=node_b2, node_gain=node_gain, node_shift=node_shift)


EPSILON = 1e-05

def norm_forward(pre_norm, norm_gain, norm_shift):
    average = lax.optimization_barrier(jnp.mean(pre_norm, axis=-1, keepdims=True))
    centred = pre_norm - average
    variance = lax.optimization_barrier(jnp.mean(centred * centred, axis=-1, keepdims=True))
    inverse = lax.rsqrt(variance + EPSILON)
    normed = centred * inverse
    return (normed * norm_gain + norm_shift, normed, inverse)

def norm_backward(grad_out, normed, inverse, norm_gain):
    scaled = grad_out * norm_gain
    return inverse * (scaled - lax.optimization_barrier(jnp.mean(scaled, axis=-1, keepdims=True)) - normed * lax.optimization_barrier(jnp.mean(scaled * normed, axis=-1, keepdims=True)))

def silu_slope(pre_act):
    sigmoid = jax.nn.sigmoid(pre_act)
    return sigmoid * (1.0 + pre_act * (1.0 - sigmoid))

def row_product(left, right):
    return lax.dot_general(left, right, (((0,), (0,)), ((), ())), preferred_element_type=jnp.float32)

def mlp_forward(inputs, weights):
    w_first, b_first, w_second, b_second, norm_gain, norm_shift = weights
    first_pre = jnp.dot(inputs, w_first, preferred_element_type=jnp.float32) + b_first
    hidden = jax.nn.silu(first_pre).astype(jnp.bfloat16)
    second_pre = jnp.dot(hidden, w_second, preferred_element_type=jnp.float32) + b_second
    output, normed, inverse = norm_forward(second_pre, norm_gain, norm_shift)
    return (output, (first_pre, hidden, normed, inverse))

def mlp_backward(inputs, saved, grad_out, weights):
    w_first, b_first, w_second, b_second, norm_gain, norm_shift = weights
    first_pre, hidden, normed, inverse = saved
    grad_second = norm_backward(grad_out, normed, inverse, norm_gain)
    second_low = grad_second.astype(jnp.bfloat16)
    grad_hidden = jnp.dot(second_low, w_second.T, preferred_element_type=jnp.float32)
    grad_first = grad_hidden * silu_slope(first_pre)
    first_low = grad_first.astype(jnp.bfloat16)
    grad_inputs = jnp.dot(first_low, w_first.T, preferred_element_type=jnp.float32)
    grads = (row_product(inputs, first_low), lax.optimization_barrier(jnp.sum(grad_first, axis=0)), row_product(hidden, second_low), lax.optimization_barrier(jnp.sum(grad_second, axis=0)), lax.optimization_barrier(jnp.sum(grad_out * normed, axis=0)), lax.optimization_barrier(jnp.sum(grad_out, axis=0)))
    return (grad_inputs, grads)

def device_pass(own_nodes, halo_rows, edge_feats, sender_ids, receiver_ids, live_blocks, node_grad_in, edge_grad_in, edge_weights, node_weights):
    node_rows, width = own_nodes.shape
    block_rows = sender_ids.shape[1]
    flat_edges = edge_feats.reshape(-1, width)
    flat_send = sender_ids.reshape(-1)
    flat_recv = receiver_ids.reshape(-1)
    edge_rows = flat_send.shape[0]
    live_mask = (jnp.arange(edge_rows, dtype=jnp.int32) // block_rows < live_blocks).astype(jnp.float32)[:, None]
    node_table = jnp.concatenate([own_nodes, halo_rows], axis=0)
    inputs = jnp.concatenate([flat_edges, node_table[flat_send], own_nodes[flat_recv]], axis=1)
    message, edge_saved = mlp_forward(inputs, edge_weights)
    live_message = message * live_mask
    aggregate = jnp.zeros((node_rows, width), jnp.float32).at[flat_recv].add(live_message)
    edge_out = (flat_edges.astype(jnp.float32) + live_message).astype(jnp.bfloat16)
    node_inputs = jnp.concatenate([own_nodes, aggregate.astype(jnp.bfloat16)], axis=1)
    update, node_saved = mlp_forward(node_inputs, node_weights)
    node_out = (own_nodes.astype(jnp.float32) + update).astype(jnp.bfloat16)
    node_grad = node_grad_in.astype(jnp.float32)
    grad_node_inputs, node_grads = mlp_backward(node_inputs, node_saved, node_grad, node_weights)
    flat_cot = edge_grad_in.reshape(-1, width).astype(jnp.float32)
    grad_message = live_mask * (flat_cot + grad_node_inputs[:, width:][flat_recv])
    grad_inputs, edge_grads = mlp_backward(inputs, edge_saved, grad_message, edge_weights)
    grad_edge = (flat_cot + grad_inputs[:, :width]).astype(jnp.bfloat16)
    table_grad = jnp.zeros((node_table.shape[0], width), jnp.float32).at[flat_send].add(grad_inputs[:, width:2 * width])
    recv_grad = jnp.zeros((node_rows, width), jnp.float32).at[flat_recv].add(grad_inputs[:, 2 * width:])
    local_grad = node_grad + grad_node_inputs[:, :width] + table_grad[:node_rows] + recv_grad
    flat_grads = jnp.concatenate([piece.reshape(-1) for piece in edge_grads + node_grads])
    return (node_out, edge_out.reshape(edge_feats.shape), grad_edge.reshape(edge_feats.shape), local_grad, table_grad[node_rows:], flat_grads)

def reference(nodes, edges, senders, receivers, block_count, send_rows, node_cot, edge_cot, edge_w1, edge_b1, edge_w2, edge_b2, edge_gain, edge_shift, node_w1, node_b1, node_w2, node_b2, node_gain, node_shift):
    edge_weights = (edge_w1, edge_b1, edge_w2, edge_b2, edge_gain, edge_shift)
    node_weights = (node_w1, node_b1, node_w2, node_b2, node_gain, node_shift)
    group_count = nodes.shape[0]
    width = nodes.shape[2]
    owners = jnp.arange(N_DOM, dtype=jnp.int32)[None, :, None] * NODE_DEV
    to_lower = (send_rows[:, :, 0, :] + owners).astype(jnp.int32)
    to_upper = (send_rows[:, :, 1, :] + owners).astype(jnp.int32)
    from_lower = jnp.roll(to_upper, 1, axis=1)
    from_upper = jnp.roll(to_lower, -1, axis=1)
    places = jnp.arange(N_DOM, dtype=jnp.int32)
    lower_valid = (places > 0).astype(jnp.float32)[None, :, None, None]
    upper_valid = (places < N_DOM - 1).astype(jnp.float32)[None, :, None, None]
    flat_rows = jnp.concatenate([from_lower, from_upper], axis=2).reshape(group_count, -1)
    valid = jnp.concatenate([jnp.broadcast_to(lower_valid, (group_count, N_DOM, SLOTS, 1)), jnp.broadcast_to(upper_valid, (group_count, N_DOM, SLOTS, 1))], axis=2)
    halo_all = jax.vmap(lambda node_table, row_ids: node_table[row_ids])(nodes, flat_rows)
    halo_all = (halo_all.reshape(group_count, N_DOM, 2 * SLOTS, width).astype(jnp.float32) * valid).astype(jnp.bfloat16)
    devices = group_count * N_DOM
    packed = (nodes.reshape(devices, NODE_DEV, width), halo_all.reshape(devices, 2 * SLOTS, width), edges.reshape(devices, BLOCKS, EBLOCK, width), senders.reshape(devices, BLOCKS, EBLOCK), receivers.reshape(devices, BLOCKS, EBLOCK), block_count.reshape(devices), node_cot.reshape(devices, NODE_DEV, width), edge_cot.reshape(devices, BLOCKS, EBLOCK, width))

    def run_device(device_item):
        return device_pass(*device_item, edge_weights, node_weights)
    node_out, edge_out, grad_edge, local_grad, halo_grad, device_grads = lax.map(run_device, packed)

    def scatter_back(row_ids, values):
        return jnp.zeros((N_DOM * NODE_DEV, width), jnp.float32).at[row_ids].add(values)
    masked_grad = halo_grad.reshape(group_count, N_DOM, 2 * SLOTS, width) * valid
    returned = jax.vmap(scatter_back)(flat_rows, masked_grad.reshape(group_count, -1, width))
    grad_node = (local_grad.reshape(group_count, N_DOM * NODE_DEV, width) + returned).astype(jnp.bfloat16)
    scale = 1.0 / math.sqrt(N_GRP * N_DOM * BLOCKS * EBLOCK)
    weight_grads = lax.optimization_barrier(jnp.sum(device_grads, axis=0)) * scale
    return (node_out.reshape(nodes.shape), edge_out.reshape(edges.shape), grad_node, grad_edge.reshape(edges.shape), weight_grads)
```

```python
import functools
import math

import jax
import jax.numpy as jnp
from jax import lax
from jax.experimental import pallas as pl
from jax.experimental.pallas import tpu as pltpu
from jax.sharding import PartitionSpec as P

EPSILON = 1e-05
BF = jnp.bfloat16
F32 = jnp.float32


def dot(a, b):
    return lax.dot_general(a, b, (((1,), (0,)), ((), ())), preferred_element_type=F32)


def dot_t(a, b):
    return lax.dot_general(a, b, (((1,), (1,)), ((), ())), preferred_element_type=F32)


def row_product(a, b):
    return lax.dot_general(a, b, (((0,), (0,)), ((), ())), preferred_element_type=F32)


def split(x):
    high = x.astype(BF)
    low = (x - high.astype(F32)).astype(BF)
    return high, low


def pair(x):
    return jnp.concatenate(split(x), axis=1)


def folded(x):
    half = x.shape[1] // 2
    return x[:, :half] + x[:, half:]


def norm_forward(pre_norm):
    average = jnp.mean(pre_norm, axis=-1, keepdims=True)
    centred = pre_norm - average
    variance = jnp.mean(centred * centred, axis=-1, keepdims=True)
    inverse = lax.rsqrt(variance + EPSILON)
    return centred * inverse, inverse


def norm_backward(grad_out, normed, inverse, gain):
    scaled = grad_out * gain
    return inverse * (
        scaled
        - jnp.mean(scaled, axis=-1, keepdims=True)
        - normed * jnp.mean(scaled * normed, axis=-1, keepdims=True)
    )


def slope_of(pre_act, sigmoid):
    return sigmoid * (1.0 + pre_act * (1.0 - sigmoid))


def column_sum(x):
    return jnp.sum(x, axis=0, keepdims=True)


def fill_rows(ref, ids_ref, count, width):
    for b in range(ids_ref.shape[0]):
        ids = jnp.broadcast_to(ids_ref[b : b + 1, :], (width, width)).T
        lane = lax.broadcasted_iota(jnp.int32, (width, width), 1)
        for c in range(count // width):
            ref[b * width : (b + 1) * width, c * width : (c + 1) * width] = jnp.where(
                ids == lane + c * width, 1.0, 0.0
            ).astype(BF)


def fill_columns(ref, ids_ref, count, width):
    for b in range(ids_ref.shape[0]):
        ids = ids_ref[b : b + 1, :]
        row = lax.broadcasted_iota(jnp.int32, (count, width), 0)
        ref[:, b * width : (b + 1) * width] = jnp.where(row == ids, 1.0, 0.0).astype(BF)


def kernel(
    sizes,
    count_ref, nodes_ref, edges_ref, send_ref, recv_ref, rows_ref, ncot_ref, ecot_ref,
    ew1, eb1, ew2, eb2, eg, es, nw1, nb1, nw2, nb2, ng, ns,
    node_out, edge_out, grad_node, grad_edge, weight_out,
    oh_s, oh_st, oh_r, oh_rt, oh_x, oh_xt,
    halo_out, halo_in, back_out, back_in,
    part_a, part_b, got_a, got_b, red_a, red_b, all_a, all_b,
    halo_send, halo_recv, back_send, back_recv,
    rs_send, rs_recv, ag_send, ag_recv,
):
    n_dom, n_grp, chunk, scale = sizes
    total = n_dom * n_grp
    d = lax.axis_index("dom")
    g = lax.axis_index("grp")
    rank = d * n_grp + g
    rows, width = nodes_ref.shape
    edge_rows = edges_ref.shape[0]
    slots = rows_ref.shape[1]
    lower = lax.rem(d + n_dom - 1, n_dom)
    upper = lax.rem(d + 1, n_dom)

    def target(k):
        t = lax.rem(rank + k, total)
        return t, {"dom": t // n_grp, "grp": lax.rem(t, n_grp)}

    barrier = pltpu.get_barrier_semaphore()

    def greet(k, carry):
        pl.semaphore_signal(
            barrier, inc=1, device_id=target(k)[1], device_id_type=pl.DeviceIdType.MESH
        )
        return carry

    lax.fori_loop(1, total, greet, 0)

    nodes = nodes_ref[...]
    fill_rows(oh_x, rows_ref, rows, width)
    halo_out[...] = dot(oh_x[...], nodes).astype(BF)

    pl.semaphore_wait(barrier, total - 1)

    def swap(out, into, send_sem, recv_sem):
        copies = []
        for side, neighbour in ((0, lower), (1, upper)):
            copy = pltpu.make_async_remote_copy(
                src_ref=out.at[pl.ds(side * slots, slots)],
                dst_ref=into.at[pl.ds((1 - side) * slots, slots)],
                send_sem=send_sem.at[side],
                recv_sem=recv_sem.at[1 - side],
                device_id={"dom": neighbour, "grp": g},
                device_id_type=pl.DeviceIdType.MESH,
            )
            copy.start()
            copies.append(copy)
        return copies

    halo_copies = swap(halo_out, halo_in, halo_send, halo_recv)

    fill_rows(oh_r, recv_ref, rows, width)
    fill_rows(oh_s, send_ref, rows + 2 * slots, width)
    fill_columns(oh_rt, recv_ref, rows, width)
    fill_columns(oh_st, send_ref, rows + 2 * slots, width)
    fill_columns(oh_xt, rows_ref, rows, width)

    live = (
        lax.broadcasted_iota(jnp.int32, (edge_rows, width), 0) < count_ref[0, 0] * width
    ).astype(F32)
    edges = edges_ref[...]
    at_recv = dot(oh_r[...], nodes).astype(BF)
    at_own = dot(oh_s[:, :rows], nodes)
    first = dot(edges, ew1[:width, :]) + dot(at_recv, ew1[2 * width :, :])

    for copy in halo_copies:
        copy.wait()
    from_lower = halo_in[:slots, :] * (d > 0).astype(BF)
    from_upper = halo_in[slots:, :] * (d < n_dom - 1).astype(BF)
    at_halo = dot(oh_s[:, rows : rows + slots], from_lower) + dot(
        oh_s[:, rows + slots :], from_upper
    )
    at_send = (at_own + at_halo).astype(BF)
    first = first + dot(at_send, ew1[width : 2 * width, :]) + eb1[...]
    sigmoid = lax.logistic(first)
    hidden = (first * sigmoid).astype(BF)
    slope = slope_of(first, sigmoid)
    second = dot(hidden, ew2[...]) + eb2[...]
    normed, inverse = norm_forward(second)
    message = (normed * eg[...] + es[...]) * live
    edge_out[...] = (edges.astype(F32) + message).astype(BF)
    aggregate = folded(dot(oh_rt[...], pair(message))).astype(BF)

    n_inputs = jnp.concatenate([nodes, aggregate], axis=1)
    n_first = dot(n_inputs, nw1[...]) + nb1[...]
    n_sigmoid = lax.logistic(n_first)
    n_hidden = (n_first * n_sigmoid).astype(BF)
    n_second = dot(n_hidden, nw2[...]) + nb2[...]
    n_normed, n_inverse = norm_forward(n_second)
    node_out[...] = (nodes.astype(F32) + (n_normed * ng[...] + ns[...])).astype(BF)

    n_cot = ncot_ref[...].astype(F32)
    n_g2 = norm_backward(n_cot, n_normed, n_inverse, ng[...])
    n_g2_low = n_g2.astype(BF)
    n_g1 = dot_t(n_g2_low, nw2[...]) * slope_of(n_first, n_sigmoid)
    n_g1_low = n_g1.astype(BF)
    n_dx = dot_t(n_g1_low, nw1[...])

    e_cot = ecot_ref[...].astype(F32)
    c = live * (e_cot + folded(dot(oh_r[...], pair(n_dx[:, width:]))))
    g2 = norm_backward(c, normed, inverse, eg[...])
    g2_low = g2.astype(BF)

    part_a[: 2 * width, :] = row_product(n_inputs, n_g1_low).astype(BF)
    part_a[2 * width : 3 * width, :] = row_product(n_hidden, n_g2_low).astype(BF)
    part_a[3 * width : 4 * width, :] = row_product(hidden, g2_low).astype(BF)
    if part_a.shape[0] > 4 * width:
        part_a[4 * width :, :] = jnp.zeros((part_a.shape[0] - 4 * width, width), BF)

    def scatter(part, got, which):
        def step(k, carry):
            t, device = target(k)
            pltpu.make_async_remote_copy(
                src_ref=part.at[pl.ds(pl.multiple_of(t * chunk, chunk), chunk)],
                dst_ref=got.at[pl.ds(pl.multiple_of(k * chunk, chunk), chunk)],
                send_sem=rs_send.at[which],
                recv_sem=rs_recv.at[which],
                device_id=device,
                device_id_type=pl.DeviceIdType.MESH,
            ).start()
            return carry

        lax.fori_loop(1, total, step, 0)

    def drain(ref, sem):
        span = ref.at[pl.ds(chunk, (total - 1) * chunk)]
        pltpu.make_async_copy(span, span, sem).wait()

    scatter(part_a, got_a, 0)

    g1 = dot_t(g2_low, ew2[...]) * slope
    g1_low = g1.astype(BF)
    at_table = dot(oh_st[...], g1_low)
    high, low = split(at_table[rows:, :])
    w_send = ew1[width : 2 * width, :]
    back_out[...] = (dot_t(high, w_send) + dot_t(low, w_send)).astype(BF)
    back_copies = swap(back_out, back_in, back_send, back_recv)

    part_b[:width, :] = row_product(edges, g1_low).astype(BF)
    part_b[width : 2 * width, :] = row_product(at_send, g1_low).astype(BF)
    part_b[2 * width : 3 * width, :] = row_product(at_recv, g1_low).astype(BF)
    small = jnp.concatenate(
        [
            column_sum(g1),
            column_sum(g2),
            column_sum(c * normed),
            column_sum(c),
            column_sum(n_g1),
            column_sum(n_g2),
            column_sum(n_cot * n_normed),
            column_sum(n_cot),
            jnp.zeros((part_b.shape[0] - 3 * width - 8, width), F32),
        ],
        axis=0,
    )
    part_b[3 * width :, :] = small.astype(BF)
    scatter(part_b, got_b, 1)

    grad_edge[...] = (e_cot + dot_t(g1_low, ew1[:width, :])).astype(BF)
    at_receiver = dot(oh_rt[...], g1_low)
    both = jnp.concatenate([at_table[:rows, :], at_receiver], axis=1)
    w_both = jnp.concatenate([w_send, ew1[2 * width :, :]], axis=1)
    high, low = split(both)
    local = n_cot + n_dx[:, :width] + dot_t(high, w_both) + dot_t(low, w_both)

    def reduce(part, got, red, whole, which):
        drain(got, rs_recv.at[which])
        mine = pl.ds(pl.multiple_of(rank * chunk, chunk), chunk)
        summed = part[mine, :].astype(F32)
        for k in range(1, total):
            summed = summed + got[k * chunk : (k + 1) * chunk, :].astype(F32)
        result = (summed * scale).astype(BF)
        red[...] = result
        whole[mine, :] = result

        def step(k, carry):
            pltpu.make_async_remote_copy(
                src_ref=red,
                dst_ref=whole.at[mine],
                send_sem=ag_send.at[which],
                recv_sem=ag_recv.at[which],
                device_id=target(k)[1],
                device_id_type=pl.DeviceIdType.MESH,
            ).start()
            return carry

        lax.fori_loop(1, total, step, 0)

    reduce(part_a, got_a, red_a, all_a, 0)

    for copy in back_copies:
        copy.wait()
    back_lower = back_in[:slots, :] * (d > 0).astype(BF)
    back_upper = back_in[slots:, :] * (d < n_dom - 1).astype(BF)
    returned = dot(oh_xt[:, :slots], back_lower) + dot(oh_xt[:, slots:], back_upper)
    grad_node[...] = (local + returned).astype(BF)

    reduce(part_b, got_b, red_b, all_b, 1)

    edge_size = 4 * width + 4
    drain(all_a, ag_recv.at[0])
    weight_out[edge_size : edge_size + 2 * width, :] = all_a[: 2 * width, :].astype(F32)
    at = edge_size + 2 * width + 1
    weight_out[at : at + width, :] = all_a[2 * width : 3 * width, :].astype(F32)
    at = 3 * width + 1
    weight_out[at : at + width, :] = all_a[3 * width : 4 * width, :].astype(F32)
    drain(all_b, ag_recv.at[1])
    weight_out[: 3 * width, :] = all_b[: 3 * width, :].astype(F32)
    small = all_b[3 * width : 3 * width + 16, :].astype(F32)
    weight_out[3 * width : 3 * width + 1, :] = small[0:1, :]
    weight_out[4 * width + 1 : 4 * width + 4, :] = small[1:4, :]
    weight_out[edge_size + 2 * width : edge_size + 2 * width + 1, :] = small[4:5, :]
    weight_out[edge_size + 3 * width + 1 : edge_size + 3 * width + 4, :] = small[5:8, :]

    drain(got_a, rs_send.at[0])
    drain(got_b, rs_send.at[1])
    drain(all_a, ag_send.at[0])
    drain(all_b, ag_send.at[1])


def shards(
    nodes, edges, senders, receivers, block_count, send_rows, node_cot, edge_cot,
    edge_w1, edge_b1, edge_w2, edge_b2, edge_gain, edge_shift,
    node_w1, node_b1, node_w2, node_b2, node_gain, node_shift,
):
    n_dom, n_grp = lax.axis_size("dom"), lax.axis_size("grp")
    total = n_dom * n_grp
    _, rows, width = nodes.shape
    _, blocks, block_rows, _ = edges.shape
    edge_rows = blocks * block_rows
    slots = send_rows.shape[3]
    chunk = -(-4 * width // (16 * total)) * 16
    padded = chunk * total
    scale = 1.0 / math.sqrt(total * edge_rows)
    vmem = pl.BlockSpec(memory_space=pltpu.VMEM)
    line = lambda v: v.reshape(1, -1)
    grads = 2 * (4 + width) * width + (3 + 2) * width * width
    sem = pltpu.SemaphoreType.DMA((2,))
    table = rows + 2 * slots
    node_out, edge_out, grad_node, grad_edge, weights = pl.pallas_call(
        functools.partial(kernel, (n_dom, n_grp, chunk, scale)),
        out_shape=(
            jax.ShapeDtypeStruct((rows, width), BF),
            jax.ShapeDtypeStruct((edge_rows, width), BF),
            jax.ShapeDtypeStruct((rows, width), BF),
            jax.ShapeDtypeStruct((edge_rows, width), BF),
            jax.ShapeDtypeStruct((grads // width, width), F32),
        ),
        in_specs=[pl.BlockSpec(memory_space=pltpu.SMEM)] + [vmem] * 19,
        out_specs=[vmem] * 5,
        scratch_shapes=[
            pltpu.VMEM((edge_rows, table), BF),
            pltpu.VMEM((table, edge_rows), BF),
            pltpu.VMEM((edge_rows, rows), BF),
            pltpu.VMEM((rows, edge_rows), BF),
            pltpu.VMEM((2 * slots, rows), BF),
            pltpu.VMEM((rows, 2 * slots), BF),
        ]
        + [pltpu.VMEM((2 * slots, width), BF)] * 4
        + [pltpu.VMEM((padded, width), BF)] * 4
        + [pltpu.VMEM((chunk, width), BF)] * 2
        + [pltpu.VMEM((padded, width), BF)] * 2
        + [sem] * 8,
        compiler_params=pltpu.CompilerParams(collective_id=0, has_side_effects=True),
    )(
        block_count,
        nodes[0],
        edges.reshape(edge_rows, width),
        senders[0],
        receivers[0],
        send_rows.reshape(2, slots),
        node_cot[0],
        edge_cot.reshape(edge_rows, width),
        edge_w1, line(edge_b1), edge_w2, line(edge_b2), line(edge_gain), line(edge_shift),
        node_w1, line(node_b1), node_w2, line(node_b2), line(node_gain), line(node_shift),
    )
    return (
        node_out[None],
        edge_out.reshape(edges.shape),
        grad_node[None],
        grad_edge.reshape(edges.shape),
        weights.reshape(-1),
    )


def solution(mesh):
    by_node = P("grp", "dom", None)
    by_edge = P("grp", "dom", None, None)
    return jax.shard_map(
        shards,
        mesh=mesh,
        in_specs=(
            by_node, by_edge, by_node, by_node, P("grp", "dom"), by_edge, by_node, by_edge,
        )
        + (P(),) * 12,
        out_specs=(by_node, by_edge, by_node, by_edge, P()),
        check_vma=False,
    )
```

```python
import functools
import math

import jax
import jax.numpy as jnp
from jax import lax
from jax.experimental import pallas as pl
from jax.experimental.pallas import tpu as pltpu
from jax.sharding import PartitionSpec as P

EPSILON = 1e-05
BF = jnp.bfloat16
F32 = jnp.float32


def dot(a, b):
    return lax.dot_general(a, b, (((1,), (0,)), ((), ())), preferred_element_type=F32)


def dot_t(a, b):
    return lax.dot_general(a, b, (((1,), (1,)), ((), ())), preferred_element_type=F32)


def row_product(a, b):
    return lax.dot_general(a, b, (((0,), (0,)), ((), ())), preferred_element_type=F32)


def split(x):
    high = x.astype(BF)
    low = (x - high.astype(F32)).astype(BF)
    return high, low


def pair(x):
    return jnp.concatenate(split(x), axis=1)


def folded(x):
    half = x.shape[1] // 2
    return x[:, :half] + x[:, half:]


def norm_forward(pre_norm):
    average = jnp.mean(pre_norm, axis=-1, keepdims=True)
    centred = pre_norm - average
    variance = jnp.mean(centred * centred, axis=-1, keepdims=True)
    inverse = lax.rsqrt(variance + EPSILON)
    return centred * inverse, inverse


def norm_backward(grad_out, normed, inverse, gain):
    scaled = grad_out * gain
    return inverse * (
        scaled
        - jnp.mean(scaled, axis=-1, keepdims=True)
        - normed * jnp.mean(scaled * normed, axis=-1, keepdims=True)
    )


def slope_of(pre_act, sigmoid):
    return sigmoid * (1.0 + pre_act * (1.0 - sigmoid))


def column_sum(x):
    return jnp.sum(x, axis=0, keepdims=True)


def fill_rows(ref, ids_ref, count, width):
    for b in range(ids_ref.shape[0]):
        ids = jnp.broadcast_to(ids_ref[b : b + 1, :], (width, width)).T
        lane = lax.broadcasted_iota(jnp.int32, (width, width), 1)
        for c in range(count // width):
            ref[b * width : (b + 1) * width, c * width : (c + 1) * width] = jnp.where(
                ids == lane + c * width, 1.0, 0.0
            ).astype(BF)


def fill_columns(ref, ids_ref, count, width):
    for b in range(ids_ref.shape[0]):
        ids = ids_ref[b : b + 1, :]
        row = lax.broadcasted_iota(jnp.int32, (count, width), 0)
        ref[:, b * width : (b + 1) * width] = jnp.where(row == ids, 1.0, 0.0).astype(BF)


def kernel(
    sizes,
    count_ref, nodes_ref, edges_ref, send_ref, recv_ref, rows_ref, ncot_ref, ecot_ref,
    ew1, eb1, ew2, eb2, eg, es, nw1, nb1, nw2, nb2, ng, ns,
    node_out, edge_out, grad_node, grad_edge, weight_out,
    oh_s, oh_st, oh_r, oh_rt, oh_x, oh_xt,
    count_here, count_sem, part_first, part_send, halo_out, halo_in, back_out, back_in,
    part_a, part_b, got_a, got_b, red_a, red_b, all_a, all_b,
    halo_send, halo_recv, back_send, back_recv,
    rs_send, rs_recv, ag_send, ag_recv,
):
    n_dom, n_grp, chunk, scale = sizes
    total = n_dom * n_grp
    d = lax.axis_index("dom")
    g = lax.axis_index("grp")
    rank = d * n_grp + g
    rows, width = nodes_ref.shape
    edge_rows = edges_ref.shape[0]
    slots = rows_ref.shape[1]
    lower = lax.rem(d + n_dom - 1, n_dom)
    upper = lax.rem(d + 1, n_dom)

    def target(k):
        t = lax.rem(rank + k, total)
        return t, {"dom": t // n_grp, "grp": lax.rem(t, n_grp)}

    count_copy = pltpu.make_async_copy(count_ref, count_here, count_sem)
    count_copy.start()
    barrier = pltpu.get_barrier_semaphore()

    def greet(k, carry):
        pl.semaphore_signal(
            barrier, inc=1, device_id=target(k)[1], device_id_type=pl.DeviceIdType.MESH
        )
        return carry

    lax.fori_loop(1, total, greet, 0)

    nodes = nodes_ref[...]
    fill_rows(oh_x, rows_ref, rows, width)
    halo_out[...] = dot(oh_x[...], nodes).astype(BF)

    has_lower = d > 0
    has_upper = d < n_dom - 1

    def swap(out, into, send_sem, recv_sem, act):
        for side, neighbour, there in ((0, lower, has_lower), (1, upper, has_upper)):
            copy = pltpu.make_async_remote_copy(
                src_ref=out.at[pl.ds(side * slots, slots)],
                dst_ref=into.at[pl.ds((1 - side) * slots, slots)],
                send_sem=send_sem.at[side],
                recv_sem=recv_sem.at[1 - side],
                device_id={"dom": neighbour, "grp": g},
                device_id_type=pl.DeviceIdType.MESH,
            )
            back = pltpu.make_async_remote_copy(
                src_ref=out.at[pl.ds((1 - side) * slots, slots)],
                dst_ref=into.at[pl.ds(side * slots, slots)],
                send_sem=send_sem.at[1 - side],
                recv_sem=recv_sem.at[side],
                device_id={"dom": neighbour, "grp": g},
                device_id_type=pl.DeviceIdType.MESH,
            )

            @pl.when(there)
            def _(copy=copy, back=back):
                if act == "start":
                    copy.start()
                else:
                    copy.wait_send()
                    back.wait_recv()

            if act == "start":

                @pl.when(jnp.logical_not(there))
                def _(side=side):
                    into[side * slots : (side + 1) * slots, :] = jnp.zeros(
                        (slots, into.shape[1]), BF
                    )


    fill_rows(oh_r, recv_ref, rows, width)
    fill_rows(oh_s, send_ref, rows + 2 * slots, width)
    fill_columns(oh_rt, recv_ref, rows, width)
    fill_columns(oh_st, send_ref, rows + 2 * slots, width)
    fill_columns(oh_xt, rows_ref, rows, width)

    count_copy.wait()
    live = (
        lax.broadcasted_iota(jnp.int32, (edge_rows, width), 0) < count_here[0, 0] * width
    ).astype(F32)
    edges = edges_ref[...]
    at_recv = dot(oh_r[...], nodes).astype(BF)
    at_own = dot(oh_s[:, :rows], nodes)
    first = dot(edges, ew1[:width, :]) + dot(at_recv, ew1[2 * width :, :])

    part_first[...] = first
    part_send[...] = at_own

    pl.semaphore_wait(barrier, total - 1)
    swap(halo_out, halo_in, halo_send, halo_recv, "start")
    swap(halo_out, halo_in, halo_send, halo_recv, "wait")
    at_send = (part_send[...] + dot(oh_s[:, rows:], halo_in[...])).astype(BF)
    first = part_first[...]
    first = first + dot(at_send, ew1[width : 2 * width, :]) + eb1[...]
    sigmoid = lax.logistic(first)
    hidden = (first * sigmoid).astype(BF)
    slope = slope_of(first, sigmoid)
    second = dot(hidden, ew2[...]) + eb2[...]
    normed, inverse = norm_forward(second)
    message = (normed * eg[...] + es[...]) * live
    edge_out[...] = (edges.astype(F32) + message).astype(BF)
    aggregate = folded(dot(oh_rt[...], pair(message))).astype(BF)

    n_inputs = jnp.concatenate([nodes, aggregate], axis=1)
    n_first = dot(n_inputs, nw1[...]) + nb1[...]
    n_sigmoid = lax.logistic(n_first)
    n_hidden = (n_first * n_sigmoid).astype(BF)
    n_second = dot(n_hidden, nw2[...]) + nb2[...]
    n_normed, n_inverse = norm_forward(n_second)
    node_out[...] = (nodes.astype(F32) + (n_normed * ng[...] + ns[...])).astype(BF)

    n_cot = ncot_ref[...].astype(F32)
    n_g2 = norm_backward(n_cot, n_normed, n_inverse, ng[...])
    n_g2_low = n_g2.astype(BF)
    n_g1 = dot_t(n_g2_low, nw2[...]) * slope_of(n_first, n_sigmoid)
    n_g1_low = n_g1.astype(BF)
    n_dx = dot_t(n_g1_low, nw1[...])

    e_cot = ecot_ref[...].astype(F32)
    c = live * (e_cot + folded(dot(oh_r[...], pair(n_dx[:, width:]))))
    g2 = norm_backward(c, normed, inverse, eg[...])
    g2_low = g2.astype(BF)

    part_a[: 2 * width, :] = row_product(n_inputs, n_g1_low).astype(BF)
    part_a[2 * width : 3 * width, :] = row_product(n_hidden, n_g2_low).astype(BF)
    part_a[3 * width : 4 * width, :] = row_product(hidden, g2_low).astype(BF)
    if part_a.shape[0] > 4 * width:
        part_a[4 * width :, :] = jnp.zeros((part_a.shape[0] - 4 * width, width), BF)

    def scatter(part, got, which):
        def step(k, carry):
            t, device = target(k)
            pltpu.make_async_remote_copy(
                src_ref=part.at[pl.ds(pl.multiple_of(t * chunk, chunk), chunk)],
                dst_ref=got.at[pl.ds(pl.multiple_of(k * chunk, chunk), chunk)],
                send_sem=rs_send.at[which],
                recv_sem=rs_recv.at[which],
                device_id=device,
                device_id_type=pl.DeviceIdType.MESH,
            ).start()
            return carry

        lax.fori_loop(1, total, step, 0)

    def drain(ref, sem):
        span = ref.at[pl.ds(chunk, (total - 1) * chunk)]
        pltpu.make_async_copy(span, span, sem).wait()

    scatter(part_a, got_a, 0)

    g1 = dot_t(g2_low, ew2[...]) * slope
    g1_low = g1.astype(BF)
    at_table = dot(oh_st[...], g1_low)
    high, low = split(at_table[rows:, :])
    w_send = ew1[width : 2 * width, :]
    back_out[...] = (dot_t(high, w_send) + dot_t(low, w_send)).astype(BF)
    swap(back_out, back_in, back_send, back_recv, "start")

    part_b[:width, :] = row_product(edges, g1_low).astype(BF)
    part_b[width : 2 * width, :] = row_product(at_send, g1_low).astype(BF)
    part_b[2 * width : 3 * width, :] = row_product(at_recv, g1_low).astype(BF)
    small = jnp.concatenate(
        [
            column_sum(g1),
            column_sum(g2),
            column_sum(c * normed),
            column_sum(c),
            column_sum(n_g1),
            column_sum(n_g2),
            column_sum(n_cot * n_normed),
            column_sum(n_cot),
            jnp.zeros((part_b.shape[0] - 3 * width - 8, width), F32),
        ],
        axis=0,
    )
    part_b[3 * width :, :] = small.astype(BF)
    scatter(part_b, got_b, 1)

    grad_edge[...] = (e_cot + dot_t(g1_low, ew1[:width, :])).astype(BF)
    at_receiver = dot(oh_rt[...], g1_low)
    both = jnp.concatenate([at_table[:rows, :], at_receiver], axis=1)
    w_both = jnp.concatenate([w_send, ew1[2 * width :, :]], axis=1)
    high, low = split(both)
    local = n_cot + n_dx[:, :width] + dot_t(high, w_both) + dot_t(low, w_both)

    def reduce(part, got, red, whole, which):
        drain(got, rs_recv.at[which])
        mine = pl.ds(pl.multiple_of(rank * chunk, chunk), chunk)
        summed = part[mine, :].astype(F32)
        for k in range(1, total):
            summed = summed + got[k * chunk : (k + 1) * chunk, :].astype(F32)
        result = (summed * scale).astype(BF)
        red[...] = result
        whole[mine, :] = result

        def step(k, carry):
            pltpu.make_async_remote_copy(
                src_ref=red,
                dst_ref=whole.at[mine],
                send_sem=ag_send.at[which],
                recv_sem=ag_recv.at[which],
                device_id=target(k)[1],
                device_id_type=pl.DeviceIdType.MESH,
            ).start()
            return carry

        lax.fori_loop(1, total, step, 0)

    reduce(part_a, got_a, red_a, all_a, 0)

    swap(back_out, back_in, back_send, back_recv, "wait")
    returned = dot(oh_xt[...], back_in[...])
    grad_node[...] = (local + returned).astype(BF)

    reduce(part_b, got_b, red_b, all_b, 1)

    edge_size = 4 * width + 4
    drain(all_a, ag_recv.at[0])
    weight_out[edge_size : edge_size + 2 * width, :] = all_a[: 2 * width, :].astype(F32)
    at = edge_size + 2 * width + 1
    weight_out[at : at + width, :] = all_a[2 * width : 3 * width, :].astype(F32)
    at = 3 * width + 1
    weight_out[at : at + width, :] = all_a[3 * width : 4 * width, :].astype(F32)
    drain(all_b, ag_recv.at[1])
    weight_out[: 3 * width, :] = all_b[: 3 * width, :].astype(F32)
    small = all_b[3 * width : 3 * width + 16, :].astype(F32)
    weight_out[3 * width : 3 * width + 1, :] = small[0:1, :]
    weight_out[4 * width + 1 : 4 * width + 4, :] = small[1:4, :]
    weight_out[edge_size + 2 * width : edge_size + 2 * width + 1, :] = small[4:5, :]
    weight_out[edge_size + 3 * width + 1 : edge_size + 3 * width + 4, :] = small[5:8, :]

    drain(got_a, rs_send.at[0])
    drain(got_b, rs_send.at[1])
    drain(all_a, ag_send.at[0])
    drain(all_b, ag_send.at[1])


def put_out(*refs):
    copies = [
        pltpu.make_async_copy(refs[i], refs[5 + i], refs[10].at[i]) for i in range(5)
    ]
    for copy in copies:
        copy.start()
    for copy in copies:
        copy.wait()


def shards(
    nodes, edges, senders, receivers, block_count, send_rows, node_cot, edge_cot,
    edge_w1, edge_b1, edge_w2, edge_b2, edge_gain, edge_shift,
    node_w1, node_b1, node_w2, node_b2, node_gain, node_shift,
):
    n_dom, n_grp = lax.axis_size("dom"), lax.axis_size("grp")
    total = n_dom * n_grp
    _, rows, width = nodes.shape
    _, blocks, block_rows, _ = edges.shape
    edge_rows = blocks * block_rows
    slots = send_rows.shape[3]
    chunk = -(-4 * width // (16 * total)) * 16
    padded = chunk * total
    scale = 1.0 / math.sqrt(total * edge_rows)
    vmem = pl.BlockSpec(memory_space=pltpu.VMEM)
    line = lambda v: v.reshape(1, -1)
    grads = 2 * (4 + width) * width + (3 + 2) * width * width
    sem = pltpu.SemaphoreType.DMA((2,))
    table = rows + 2 * slots
    results = (
        jax.ShapeDtypeStruct((rows, width), BF),
        jax.ShapeDtypeStruct((edge_rows, width), BF),
        jax.ShapeDtypeStruct((rows, width), BF),
        jax.ShapeDtypeStruct((edge_rows, width), BF),
        jax.ShapeDtypeStruct((grads // width, width), F32),
    )
    held = pl.pallas_call(
        functools.partial(kernel, (n_dom, n_grp, chunk, scale)),
        out_shape=tuple(pltpu.VMEM(v.shape, v.dtype) for v in results),
        in_specs=[pl.BlockSpec(memory_space=pltpu.HBM)] + [vmem] * 19,
        out_specs=[vmem] * 5,
        scratch_shapes=[
            pltpu.VMEM((edge_rows, table), BF),
            pltpu.VMEM((table, edge_rows), BF),
            pltpu.VMEM((edge_rows, rows), BF),
            pltpu.VMEM((rows, edge_rows), BF),
            pltpu.VMEM((2 * slots, rows), BF),
            pltpu.VMEM((rows, 2 * slots), BF),
        ]
        + [pltpu.SMEM((1, 1), jnp.int32), pltpu.SemaphoreType.DMA]
        + [pltpu.VMEM((edge_rows, width), F32)] * 2
        + [pltpu.VMEM((2 * slots, width), BF)] * 4
        + [pltpu.VMEM((padded, width), BF)] * 4
        + [pltpu.VMEM((chunk, width), BF)] * 2
        + [pltpu.VMEM((padded, width), BF)] * 2
        + [sem] * 8,
        compiler_params=pltpu.CompilerParams(collective_id=0, has_side_effects=True),
    )(
        block_count,
        nodes[0],
        edges.reshape(edge_rows, width),
        senders[0],
        receivers[0],
        send_rows.reshape(2, slots),
        node_cot[0],
        edge_cot.reshape(edge_rows, width),
        edge_w1, line(edge_b1), edge_w2, line(edge_b2), line(edge_gain), line(edge_shift),
        node_w1, line(node_b1), node_w2, line(node_b2), line(node_gain), line(node_shift),
    )
    node_out, edge_out, grad_node, grad_edge, weights = pl.pallas_call(
        put_out,
        out_shape=results,
        in_specs=[vmem] * 5,
        out_specs=[pl.BlockSpec(memory_space=pl.ANY)] * 5,
        scratch_shapes=[pltpu.SemaphoreType.DMA((5,))],
    )(*(pltpu.with_memory_space_constraint(v, pltpu.VMEM) for v in held))
    return (
        node_out[None],
        edge_out.reshape(edges.shape),
        grad_node[None],
        grad_edge.reshape(edges.shape),
        weights.reshape(-1),
    )


def solution(mesh):
    by_node = P("grp", "dom", None)
    by_edge = P("grp", "dom", None, None)
    return jax.shard_map(
        shards,
        mesh=mesh,
        in_specs=(
            by_node, by_edge, by_node, by_node, P("grp", "dom"), by_edge, by_node, by_edge,
        )
        + (P(),) * 12,
        out_specs=(by_node, by_edge, by_node, by_edge, P()),
        check_vma=False,
    )
```

```python
import functools
import math

import jax
import jax.numpy as jnp
from jax import lax
from jax.experimental import pallas as pl
from jax.experimental.pallas import tpu as pltpu
from jax.sharding import PartitionSpec as P

EPSILON = 1e-05
BF = jnp.bfloat16
F32 = jnp.float32


def dot(a, b):
    return lax.dot_general(a, b, (((1,), (0,)), ((), ())), preferred_element_type=F32)


def dot_t(a, b):
    return lax.dot_general(a, b, (((1,), (1,)), ((), ())), preferred_element_type=F32)


def row_product(a, b):
    return lax.dot_general(a, b, (((0,), (0,)), ((), ())), preferred_element_type=F32)


def split(x):
    high = x.astype(BF)
    low = (x - high.astype(F32)).astype(BF)
    return high, low


def pair(x):
    return jnp.concatenate(split(x), axis=1)


def folded(x):
    half = x.shape[1] // 2
    return x[:, :half] + x[:, half:]


def norm_forward(pre_norm):
    average = jnp.mean(pre_norm, axis=-1, keepdims=True)
    centred = pre_norm - average
    variance = jnp.mean(centred * centred, axis=-1, keepdims=True)
    inverse = lax.rsqrt(variance + EPSILON)
    return centred * inverse, inverse


def norm_backward(grad_out, normed, inverse, gain):
    scaled = grad_out * gain
    return inverse * (
        scaled
        - jnp.mean(scaled, axis=-1, keepdims=True)
        - normed * jnp.mean(scaled * normed, axis=-1, keepdims=True)
    )


def slope_of(pre_act, sigmoid):
    return sigmoid * (1.0 + pre_act * (1.0 - sigmoid))


def column_sum(x):
    return jnp.sum(x, axis=0, keepdims=True)


def fill_rows(ref, ids_ref, count, width):
    for b in range(ids_ref.shape[0]):
        ids = jnp.broadcast_to(ids_ref[b : b + 1, :], (width, width)).T
        lane = lax.broadcasted_iota(jnp.int32, (width, width), 1)
        for c in range(count // width):
            ref[b * width : (b + 1) * width, c * width : (c + 1) * width] = jnp.where(
                ids == lane + c * width, 1.0, 0.0
            ).astype(BF)


def fill_columns(ref, ids_ref, count, width):
    for b in range(ids_ref.shape[0]):
        ids = ids_ref[b : b + 1, :]
        row = lax.broadcasted_iota(jnp.int32, (count, width), 0)
        ref[:, b * width : (b + 1) * width] = jnp.where(row == ids, 1.0, 0.0).astype(BF)


def kernel(
    sizes, *refs
):
    body(sizes, refs[:20], *refs[20:])


def body(
    sizes, operands, node_out, edge_out, grad_node, grad_edge, weight_out,
    oh_s, oh_st, oh_r, oh_rt, oh_x, oh_xt,
    held, load_sems, part_first, part_send, halo_out, halo_in, back_out, back_in,
    part_a, part_b, got_a, got_b, red_a, red_b, all_a, all_b,
    halo_send, halo_recv, back_send, back_recv,
    rs_send, rs_recv, ag_send, ag_recv,
):
    n_dom, n_grp, chunk, scale = sizes
    (
        count_here, nodes_ref, edges_ref, send_ref, recv_ref, rows_ref, ncot_ref, ecot_ref,
        ew1, eb1, ew2, eb2, eg, es, nw1, nb1, nw2, nb2, ng, ns,
    ) = held
    loads = [
        pltpu.make_async_copy(operand, ref, load_sems.at[i])
        for i, (operand, ref) in enumerate(zip(operands, held))
    ]
    early = (5, 1)
    late = [i for i in range(len(loads)) if i not in early]
    for i in early:
        loads[i].start()
    total = n_dom * n_grp
    d = lax.axis_index("dom")
    g = lax.axis_index("grp")
    rank = d * n_grp + g
    rows, width = nodes_ref.shape
    edge_rows = edges_ref.shape[0]
    slots = rows_ref.shape[1]
    lower = lax.rem(d + n_dom - 1, n_dom)
    upper = lax.rem(d + 1, n_dom)

    def target(k):
        t = lax.rem(rank + k, total)
        return t, {"dom": t // n_grp, "grp": lax.rem(t, n_grp)}

    barrier = pltpu.get_barrier_semaphore()

    def greet(k, carry):
        pl.semaphore_signal(
            barrier, inc=1, device_id=target(k)[1], device_id_type=pl.DeviceIdType.MESH
        )
        return carry

    lax.fori_loop(1, total, greet, 0)
    for i in late:
        loads[i].start()
    for i in early:
        loads[i].wait()

    nodes = nodes_ref[...]
    fill_rows(oh_x, rows_ref, rows, width)
    halo_out[...] = dot(oh_x[...], nodes).astype(BF)

    has_lower = d > 0
    has_upper = d < n_dom - 1

    def swap(out, into, send_sem, recv_sem, act):
        for side, neighbour, there in ((0, lower, has_lower), (1, upper, has_upper)):
            copy = pltpu.make_async_remote_copy(
                src_ref=out.at[pl.ds(side * slots, slots)],
                dst_ref=into.at[pl.ds((1 - side) * slots, slots)],
                send_sem=send_sem.at[side],
                recv_sem=recv_sem.at[1 - side],
                device_id={"dom": neighbour, "grp": g},
                device_id_type=pl.DeviceIdType.MESH,
            )
            back = pltpu.make_async_remote_copy(
                src_ref=out.at[pl.ds((1 - side) * slots, slots)],
                dst_ref=into.at[pl.ds(side * slots, slots)],
                send_sem=send_sem.at[1 - side],
                recv_sem=recv_sem.at[side],
                device_id={"dom": neighbour, "grp": g},
                device_id_type=pl.DeviceIdType.MESH,
            )

            @pl.when(there)
            def _(copy=copy, back=back):
                if act == "start":
                    copy.start()
                else:
                    copy.wait_send()
                    back.wait_recv()

            if act == "start":

                @pl.when(jnp.logical_not(there))
                def _(side=side):
                    into[side * slots : (side + 1) * slots, :] = jnp.zeros(
                        (slots, into.shape[1]), BF
                    )


    for i in late:
        loads[i].wait()
    fill_rows(oh_r, recv_ref, rows, width)
    fill_rows(oh_s, send_ref, rows + 2 * slots, width)
    fill_columns(oh_rt, recv_ref, rows, width)
    fill_columns(oh_st, send_ref, rows + 2 * slots, width)
    fill_columns(oh_xt, rows_ref, rows, width)

    live = (
        lax.broadcasted_iota(jnp.int32, (edge_rows, width), 0) < count_here[0, 0] * width
    ).astype(F32)
    edges = edges_ref[...]
    at_recv = dot(oh_r[...], nodes).astype(BF)
    at_own = dot(oh_s[:, :rows], nodes)
    first = dot(edges, ew1[:width, :]) + dot(at_recv, ew1[2 * width :, :])

    part_first[...] = first
    part_send[...] = at_own

    pl.semaphore_wait(barrier, total - 1)
    swap(halo_out, halo_in, halo_send, halo_recv, "start")
    swap(halo_out, halo_in, halo_send, halo_recv, "wait")
    at_send = (part_send[...] + dot(oh_s[:, rows:], halo_in[...])).astype(BF)
    first = part_first[...]
    first = first + dot(at_send, ew1[width : 2 * width, :]) + eb1[...]
    sigmoid = lax.logistic(first)
    hidden = (first * sigmoid).astype(BF)
    slope = slope_of(first, sigmoid)
    second = dot(hidden, ew2[...]) + eb2[...]
    normed, inverse = norm_forward(second)
    message = (normed * eg[...] + es[...]) * live
    edge_out[...] = (edges.astype(F32) + message).astype(BF)
    aggregate = folded(dot(oh_rt[...], pair(message))).astype(BF)

    n_inputs = jnp.concatenate([nodes, aggregate], axis=1)
    n_first = dot(n_inputs, nw1[...]) + nb1[...]
    n_sigmoid = lax.logistic(n_first)
    n_hidden = (n_first * n_sigmoid).astype(BF)
    n_second = dot(n_hidden, nw2[...]) + nb2[...]
    n_normed, n_inverse = norm_forward(n_second)
    node_out[...] = (nodes.astype(F32) + (n_normed * ng[...] + ns[...])).astype(BF)

    n_cot = ncot_ref[...].astype(F32)
    n_g2 = norm_backward(n_cot, n_normed, n_inverse, ng[...])
    n_g2_low = n_g2.astype(BF)
    n_g1 = dot_t(n_g2_low, nw2[...]) * slope_of(n_first, n_sigmoid)
    n_g1_low = n_g1.astype(BF)
    n_dx = dot_t(n_g1_low, nw1[...])

    e_cot = ecot_ref[...].astype(F32)
    c = live * (e_cot + folded(dot(oh_r[...], pair(n_dx[:, width:]))))
    g2 = norm_backward(c, normed, inverse, eg[...])
    g2_low = g2.astype(BF)

    part_a[: 2 * width, :] = row_product(n_inputs, n_g1_low).astype(BF)
    part_a[2 * width : 3 * width, :] = row_product(n_hidden, n_g2_low).astype(BF)
    part_a[3 * width : 4 * width, :] = row_product(hidden, g2_low).astype(BF)
    if part_a.shape[0] > 4 * width:
        part_a[4 * width :, :] = jnp.zeros((part_a.shape[0] - 4 * width, width), BF)

    def scatter(part, got, which):
        def step(k, carry):
            t, device = target(k)
            pltpu.make_async_remote_copy(
                src_ref=part.at[pl.ds(pl.multiple_of(t * chunk, chunk), chunk)],
                dst_ref=got.at[pl.ds(pl.multiple_of(k * chunk, chunk), chunk)],
                send_sem=rs_send.at[which],
                recv_sem=rs_recv.at[which],
                device_id=device,
                device_id_type=pl.DeviceIdType.MESH,
            ).start()
            return carry

        lax.fori_loop(1, total, step, 0)

    def drain(ref, sem):
        span = ref.at[pl.ds(chunk, (total - 1) * chunk)]
        pltpu.make_async_copy(span, span, sem).wait()

    scatter(part_a, got_a, 0)

    g1 = dot_t(g2_low, ew2[...]) * slope
    g1_low = g1.astype(BF)
    at_table = dot(oh_st[...], g1_low)
    high, low = split(at_table[rows:, :])
    w_send = ew1[width : 2 * width, :]
    back_out[...] = (dot_t(high, w_send) + dot_t(low, w_send)).astype(BF)
    swap(back_out, back_in, back_send, back_recv, "start")

    part_b[:width, :] = row_product(edges, g1_low).astype(BF)
    part_b[width : 2 * width, :] = row_product(at_send, g1_low).astype(BF)
    part_b[2 * width : 3 * width, :] = row_product(at_recv, g1_low).astype(BF)
    small = jnp.concatenate(
        [
            column_sum(g1),
            column_sum(g2),
            column_sum(c * normed),
            column_sum(c),
            column_sum(n_g1),
            column_sum(n_g2),
            column_sum(n_cot * n_normed),
            column_sum(n_cot),
            jnp.zeros((part_b.shape[0] - 3 * width - 8, width), F32),
        ],
        axis=0,
    )
    part_b[3 * width :, :] = small.astype(BF)
    scatter(part_b, got_b, 1)

    grad_edge[...] = (e_cot + dot_t(g1_low, ew1[:width, :])).astype(BF)
    at_receiver = dot(oh_rt[...], g1_low)
    both = jnp.concatenate([at_table[:rows, :], at_receiver], axis=1)
    w_both = jnp.concatenate([w_send, ew1[2 * width :, :]], axis=1)
    high, low = split(both)
    local = n_cot + n_dx[:, :width] + dot_t(high, w_both) + dot_t(low, w_both)

    def reduce(part, got, red, whole, which):
        drain(got, rs_recv.at[which])
        mine = pl.ds(pl.multiple_of(rank * chunk, chunk), chunk)
        summed = part[mine, :].astype(F32)
        for k in range(1, total):
            summed = summed + got[k * chunk : (k + 1) * chunk, :].astype(F32)
        result = (summed * scale).astype(BF)
        red[...] = result
        whole[mine, :] = result

        def step(k, carry):
            pltpu.make_async_remote_copy(
                src_ref=red,
                dst_ref=whole.at[mine],
                send_sem=ag_send.at[which],
                recv_sem=ag_recv.at[which],
                device_id=target(k)[1],
                device_id_type=pl.DeviceIdType.MESH,
            ).start()
            return carry

        lax.fori_loop(1, total, step, 0)

    reduce(part_a, got_a, red_a, all_a, 0)

    swap(back_out, back_in, back_send, back_recv, "wait")
    returned = dot(oh_xt[...], back_in[...])
    grad_node[...] = (local + returned).astype(BF)

    reduce(part_b, got_b, red_b, all_b, 1)

    edge_size = 4 * width + 4
    drain(all_a, ag_recv.at[0])
    weight_out[edge_size : edge_size + 2 * width, :] = all_a[: 2 * width, :].astype(F32)
    at = edge_size + 2 * width + 1
    weight_out[at : at + width, :] = all_a[2 * width : 3 * width, :].astype(F32)
    at = 3 * width + 1
    weight_out[at : at + width, :] = all_a[3 * width : 4 * width, :].astype(F32)
    drain(all_b, ag_recv.at[1])
    weight_out[: 3 * width, :] = all_b[: 3 * width, :].astype(F32)
    small = all_b[3 * width : 3 * width + 16, :].astype(F32)
    weight_out[3 * width : 3 * width + 1, :] = small[0:1, :]
    weight_out[4 * width + 1 : 4 * width + 4, :] = small[1:4, :]
    weight_out[edge_size + 2 * width : edge_size + 2 * width + 1, :] = small[4:5, :]
    weight_out[edge_size + 3 * width + 1 : edge_size + 3 * width + 4, :] = small[5:8, :]

    drain(got_a, rs_send.at[0])
    drain(got_b, rs_send.at[1])
    drain(all_a, ag_send.at[0])
    drain(all_b, ag_send.at[1])


def put_out(*refs):
    copies = [
        pltpu.make_async_copy(refs[i], refs[5 + i], refs[10].at[i]) for i in range(5)
    ]
    for copy in copies:
        copy.start()
    for copy in copies:
        copy.wait()


def shards(
    nodes, edges, senders, receivers, block_count, send_rows, node_cot, edge_cot,
    edge_w1, edge_b1, edge_w2, edge_b2, edge_gain, edge_shift,
    node_w1, node_b1, node_w2, node_b2, node_gain, node_shift,
):
    n_dom, n_grp = lax.axis_size("dom"), lax.axis_size("grp")
    total = n_dom * n_grp
    _, rows, width = nodes.shape
    _, blocks, block_rows, _ = edges.shape
    edge_rows = blocks * block_rows
    slots = send_rows.shape[3]
    chunk = -(-4 * width // (16 * total)) * 16
    padded = chunk * total
    scale = 1.0 / math.sqrt(total * edge_rows)
    vmem = pl.BlockSpec(memory_space=pltpu.VMEM)
    line = lambda v: v.reshape(1, -1)
    grads = 2 * (4 + width) * width + (3 + 2) * width * width
    sem = pltpu.SemaphoreType.DMA((2,))
    table = rows + 2 * slots
    operands = (
        block_count,
        nodes[0],
        edges.reshape(edge_rows, width),
        senders[0],
        receivers[0],
        send_rows.reshape(2, slots),
        node_cot[0],
        edge_cot.reshape(edge_rows, width),
        edge_w1, line(edge_b1), edge_w2, line(edge_b2), line(edge_gain), line(edge_shift),
        node_w1, line(node_b1), node_w2, line(node_b2), line(node_gain), line(node_shift),
    )
    results = (
        jax.ShapeDtypeStruct((rows, width), BF),
        jax.ShapeDtypeStruct((edge_rows, width), BF),
        jax.ShapeDtypeStruct((rows, width), BF),
        jax.ShapeDtypeStruct((edge_rows, width), BF),
        jax.ShapeDtypeStruct((grads // width, width), F32),
    )
    held = pl.pallas_call(
        functools.partial(kernel, (n_dom, n_grp, chunk, scale)),
        out_shape=tuple(pltpu.VMEM(v.shape, v.dtype) for v in results),
        in_specs=[pl.BlockSpec(memory_space=pltpu.HBM)] * len(operands),
        out_specs=[vmem] * 5,
        scratch_shapes=[
            pltpu.VMEM((edge_rows, table), BF),
            pltpu.VMEM((table, edge_rows), BF),
            pltpu.VMEM((edge_rows, rows), BF),
            pltpu.VMEM((rows, edge_rows), BF),
            pltpu.VMEM((2 * slots, rows), BF),
            pltpu.VMEM((rows, 2 * slots), BF),
        ]
        + [[pltpu.SMEM((1, 1), jnp.int32)] + [pltpu.VMEM(v.shape, v.dtype) for v in operands[1:]]]
        + [pltpu.SemaphoreType.DMA((len(operands),))]
        + [pltpu.VMEM((edge_rows, width), F32)] * 2
        + [pltpu.VMEM((2 * slots, width), BF)] * 4
        + [pltpu.VMEM((padded, width), BF)] * 4
        + [pltpu.VMEM((chunk, width), BF)] * 2
        + [pltpu.VMEM((padded, width), BF)] * 2
        + [sem] * 8,
        compiler_params=pltpu.CompilerParams(collective_id=0, has_side_effects=True),
    )(*operands)
    node_out, edge_out, grad_node, grad_edge, weights = pl.pallas_call(
        put_out,
        out_shape=results,
        in_specs=[vmem] * 5,
        out_specs=[pl.BlockSpec(memory_space=pl.ANY)] * 5,
        scratch_shapes=[pltpu.SemaphoreType.DMA((5,))],
    )(*(pltpu.with_memory_space_constraint(v, pltpu.VMEM) for v in held))
    return (
        node_out[None],
        edge_out.reshape(edges.shape),
        grad_node[None],
        grad_edge.reshape(edges.shape),
        weights.reshape(-1),
    )


def solution(mesh):
    by_node = P("grp", "dom", None)
    by_edge = P("grp", "dom", None, None)
    return jax.shard_map(
        shards,
        mesh=mesh,
        in_specs=(
            by_node, by_edge, by_node, by_node, P("grp", "dom"), by_edge, by_node, by_edge,
        )
        + (P(),) * 12,
        out_specs=(by_node, by_edge, by_node, by_edge, P()),
        check_vma=False,
    )
```
